32 devices in a mesh: src: 8 (over z, y), tm: 4 (over x, core).
Axes of the slice: x: 2, y: 2, z: 4, core: 2. Of those that a mesh axis runs over, the one named last changes fastest.
Arguments:
- green: bfloat16 [4, 1024, 128, 128], P('tm', 'src'), may hold values from -0.046875 to 0.046875
- block_rows: int32 [4, 1024], P('tm', 'src'), may hold values from 0 to 7
- block_cols: int32 [4, 1024], P('tm', 'src'), may hold values from 0 to 31
- block_live: int32 [4, 1024], P('tm', 'src'), may hold values from 0 to 1, as said below
- data: float32 [4, 1024, 128], P('tm', 'src'), may hold values from -6 to 6
- row_weight: float32 [4, 1024], P('tm', 'src'), may hold values from 0.3 to 9
- source_gain: float32 [32768], P('src'), may hold values from 0.2 to 3
Outputs:
- solution: float32 [32768, 128], P(('src', 'tm'))
- residual: float32 [4, 1024, 128], P('tm', 'src')
- misfit: float32 [2, 128], replicated
The draws below stay inside these ranges and needn't reach their ends.
Inputs may be any that keep to these rules, and one draw needn't show every extreme that they name: `block_live`: within one device's 128 slots every slot is live with the same chance, a chance that differs from device to device; in some device all 128 slots are live.
All inputs are finite; a program needn't handle non-finite values.
Results may differ from the reference program's by a relative error of at most 0.0038.
Values may be sent and summed in bfloat16 or wider, within the bound.
No kernel may reach another device: no remote copies, remote signals or barrier semaphores. Data moves between devices by JAX's collectives and lax.ppermute only.
A program may use at most 128 MiB of HBM per device.

```python
import math
import jax
import jax.numpy as jnp
from jax import lax

BS = 128
DATASETS = 128
NB = 128
ROWB_DEV = 1
ITERS = 2
WINDOWS = 4
GROUPS = 8
RB = 8
CB = 32
WROWS = 1024
ROWS = 4096
SOURCES = 32768


def draw_block_live(key, part):
    first_key, second_key, third_key = jax.random.split(key, 3)
    devices = WINDOWS * GROUPS
    levels = jax.random.randint(first_key, (devices,), 2, 9)
    chosen = jax.random.randint(second_key, (), 0, devices)
    levels = jnp.where(jnp.arange(devices, dtype=jnp.int32) == chosen, 8, levels)
    coin_flips = jax.random.randint(third_key, (devices, NB), 0, 8)
    live_slots = (coin_flips < levels[:, None]).astype(jnp.int32)
    return live_slots.reshape(WINDOWS, GROUPS * NB)


def draw_row_weight(key, part):
    count_all = WINDOWS * WROWS
    position = jnp.arange(count_all, dtype=jnp.float32) / (count_all - 1)
    rising = 1.0 + 2.0 * position
    spread = jnp.exp(jax.random.uniform(key, (count_all,), jnp.float32, math.log(0.3), math.log(3.0)))
    return (rising * spread).reshape(WINDOWS, WROWS)


def draw_source_gain(key, part):
    position = jnp.arange(SOURCES, dtype=jnp.float32) / (SOURCES - 1)
    rising = 1.0 + 2.0 * position
    spread = jnp.exp(jax.random.uniform(key, (SOURCES,), jnp.float32, math.log(0.2), 0.0))
    return rising * spread


def place_ends(array, rng, smallest, high):
    place = [jax.random.randint(jax.random.fold_in(rng, axis), (), 0, length) for axis, length in enumerate(array.shape)]
    longest = array.shape.index(max(array.shape))
    neighbour = place[:longest] + [(place[longest] + 1) % array.shape[longest]] + place[longest + 1:]
    return array.at[tuple(place)].set(smallest).at[tuple(neighbour)].set(high)


def level_of(own_key, shape, shards, smallest, largest):
    level = 1.0
    for dim, parts in shards:
        heights = jax.random.uniform(jax.random.fold_in(jax.random.fold_in(own_key, 6), dim), (parts,), jnp.float32, smallest / len(shards), largest / len(shards))
        level = level * jnp.repeat(jnp.exp(heights), shape[dim] // parts).reshape((-1,) + (1,) * (len(shape) - 1 - dim))
    return level


def gaussian(rng, shape, scale, most, pieces=(), kind=jnp.bfloat16):
    drawn = jax.random.normal(rng, shape, jnp.float32) * scale
    if len(pieces) > 0:
        drawn = level_of(rng, shape, pieces, -0.22, 0.18) * drawn
    return jnp.clip(drawn, min=-most, max=most).astype(kind)


def setup_inputs(seed: int = 0) -> dict:
    seeds = jax.random.split(jax.random.key(seed), 8)
    green = gaussian(seeds[0], (WINDOWS, GROUPS * NB, BS, BS), (BS * NB // ROWB_DEV) ** -0.5, 0.046875, ((0, 4), (1, 8)))
    block_rows = place_ends(jax.random.randint(seeds[1], (WINDOWS, GROUPS * NB), 0, RB), jax.random.fold_in(seeds[1], 1), 0, RB - 1).astype(jnp.int32)
    block_cols = place_ends(jax.random.randint(seeds[2], (WINDOWS, GROUPS * NB), 0, CB), jax.random.fold_in(seeds[2], 1), 0, CB - 1).astype(jnp.int32)
    block_live = draw_block_live(jax.random.fold_in(seeds[7], 71), 0)
    data = gaussian(seeds[4], (WINDOWS, WROWS, DATASETS), 1.0, 6.0, ((0, 4), (1, 8)), jnp.float32)
    row_weight = draw_row_weight(jax.random.fold_in(seeds[7], 71), 0)
    source_gain = draw_source_gain(jax.random.fold_in(seeds[7], 71), 0)
    return {"green": green, "block_rows": block_rows, "block_cols": block_cols, "block_live": block_live, "data": data, "row_weight": row_weight, "source_gain": source_gain}


HIGH = lax.Precision.HIGHEST
EPSILON = 1e-6


def forward_product(blocks_all, rows_all, cols_all, live_all, scaled):
    grouped = scaled.reshape(GROUPS, CB, BS, DATASETS)

    def one_window(window):
        def advance(summed, group):
            blocks = blocks_all[window, group].astype(jnp.float32)
            picked = grouped[group][cols_all[window, group]].astype(jnp.float32)
            products = jnp.einsum("kac,kcr->kar", blocks, picked, precision=HIGH)
            products = products * live_all[window, group].astype(jnp.float32)[:, None, None]
            return summed.at[rows_all[window, group]].add(products), None

        start_sum = jnp.zeros((RB, BS, DATASETS), jnp.float32)
        summed, ignored = lax.scan(advance, start_sum, jnp.arange(GROUPS, dtype=jnp.int32))
        return summed

    image = lax.map(one_window, jnp.arange(WINDOWS, dtype=jnp.int32))
    return image.reshape(WINDOWS, WROWS, DATASETS)


def adjoint_product(blocks_all, rows_all, cols_all, live_all, sent):
    row_groups = sent.reshape(WINDOWS, RB, BS, DATASETS)

    def one_group(group):
        def advance(summed, window):
            blocks = blocks_all[window, group].astype(jnp.float32)
            picked = row_groups[window][rows_all[window, group]].astype(jnp.float32)
            products = jnp.einsum("kac,kar->kcr", blocks, picked, precision=HIGH)
            products = products * live_all[window, group].astype(jnp.float32)[:, None, None]
            return summed.at[cols_all[window, group]].add(products), None

        start_sum = jnp.zeros((CB, BS, DATASETS), jnp.float32)
        summed, ignored = lax.scan(advance, start_sum, jnp.arange(WINDOWS, dtype=jnp.int32))
        return summed

    grads = lax.map(one_group, jnp.arange(GROUPS, dtype=jnp.int32))
    return grads.reshape(SOURCES, DATASETS)


def reference(green, block_rows, block_cols, block_live, data, row_weight, source_gain):
    blocks_all = green.reshape(WINDOWS, GROUPS, NB, BS, BS)
    rows_all = block_rows.reshape(WINDOWS, GROUPS, NB)
    cols_all = block_cols.reshape(WINDOWS, GROUPS, NB)
    live_all = block_live.reshape(WINDOWS, GROUPS, NB)
    weight = row_weight[:, :, None]
    gain = source_gain[:, None]
    residual = weight * data
    sent = (weight * residual).astype(jnp.bfloat16)
    steepest = gain * adjoint_product(blocks_all, rows_all, cols_all, live_all, sent)
    gamma_now = jnp.sum(steepest * steepest, axis=0)
    direction = steepest
    solution = jnp.zeros((SOURCES, DATASETS), jnp.float32)
    misfits = []
    for iteration in range(ITERS):
        scaled = (gain * direction).astype(jnp.bfloat16)
        image = weight * forward_product(blocks_all, rows_all, cols_all, live_all, scaled)
        image_norm = jnp.sum(image * image, axis=(0, 1))
        step_size = gamma_now / (image_norm + EPSILON)
        solution = solution + step_size * direction
        residual = residual - step_size * image
        misfits.append(jnp.sum(residual * residual, axis=(0, 1)) / ROWS)
        if iteration + 1 < ITERS:
            sent = (weight * residual).astype(jnp.bfloat16)
            steepest = gain * adjoint_product(blocks_all, rows_all, cols_all, live_all, sent)
            gamma_next = jnp.sum(steepest * steepest, axis=0)
            direction = steepest + (gamma_next / (gamma_now + EPSILON)) * direction
            gamma_now = gamma_next
    return solution, residual, jnp.stack(misfits)
```

```python
import jax
import jax.numpy as jnp
from jax import lax
from jax.experimental import pallas as pl
from jax.experimental.pallas import tpu as pltpu
from jax.sharding import PartitionSpec as P


ITERS = 2
EPSILON = 1e-06
PARTS = 2
BF = jnp.bfloat16
F32 = jnp.float32


def params(mib):
    return pltpu.CompilerParams(vmem_limit_bytes=mib << 20)


def sds(shape, dtype=F32):
    return jax.ShapeDtypeStruct(shape, dtype)


def xor_permute(array, axis, count, bit):
    return lax.ppermute(array, axis, [(i, i ^ bit) for i in range(count)])


def shards(green, block_rows, block_cols, block_live, data, row_weight, source_gain):
    blocks = green[0]
    slot_count, bs, _ = blocks.shape
    own_rows, ds = data.shape[1], data.shape[2]
    groups = lax.axis_size("src")
    windows = lax.axis_size("tm")
    devices = groups * windows
    sources = source_gain.shape[0]
    wrows = own_rows * groups
    row_blocks = wrows // bs
    col_blocks = sources // bs
    share = sources // windows
    share_blocks = share // bs
    total_rows = wrows * windows
    pairs = windows // 2

    def where():
        tm_index = lax.axis_index("tm")
        return [tm_index & 1, 1 - (tm_index & 1), tm_index >> 1, lax.axis_index("src")]

    gain_rows = source_gain.reshape(windows, 1, share)
    vmem = pl.BlockSpec(memory_space=pltpu.VMEM)
    hbm = pl.BlockSpec(memory_space=pltpu.HBM)

    def kernel(body, out_shape, count, placed=False, in_specs=None, scratch=(), mib=12, cost=None,
               aliases=None):
        def run(*refs):
            body(where(), *refs)

        return pl.pallas_call(
            run if placed else body,
            out_shape=out_shape,
            in_specs=[vmem] * count if in_specs is None else in_specs,
            out_specs=jax.tree.map(lambda _: vmem, out_shape),
            scratch_shapes=scratch,
            input_output_aliases=aliases or {},
            compiler_params=params(mib),
            cost_estimate=cost,
        )

    def after(array, *others):
        return lax.optimization_barrier((array, *others))[0]

    def cost_of(flops, nbytes):
        return pl.CostEstimate(flops=flops, transcendentals=0, bytes_accessed=nbytes)

    def repeat(tile, out_ref, count):
        height = tile.shape[0]
        for b in range(count):
            out_ref[b * height:(b + 1) * height, :] = tile

    def pre_body(data_hbm, w_hbm, sent_ref, r_ref, data_ref, w_ref, sem):
        copies = [
            pltpu.make_async_copy(data_hbm, data_ref, sem.at[0]),
            pltpu.make_async_copy(w_hbm, w_ref, sem.at[1]),
        ]
        for copy in copies:
            copy.start()
        for copy in copies:
            copy.wait()
        residual = w_ref[...] * jnp.transpose(data_ref[...])
        sent_ref[...] = (w_ref[...] * residual).astype(BF)
        r_ref[...] = jnp.transpose(residual)

    sent, residual0 = kernel(
        pre_body, (sds((ds, own_rows), BF), sds((own_rows, ds))), 2, in_specs=[hbm, hbm],
        scratch=[
            pltpu.VMEM((own_rows, ds), F32), pltpu.VMEM((1, own_rows), F32),
            pltpu.SemaphoreType.DMA((2,)),
        ],
    )(*[pltpu.with_memory_space_constraint(x, pltpu.HBM) for x in (data[0], row_weight)])

    own_blocks = own_rows // bs

    def place(device):
        return (device & 1) * (groups // 2) + (device >> 1)

    def split(x, size):
        assert size & (size - 1) == 0
        return x >> (size.bit_length() - 1), x & (size - 1)

    cells = row_blocks * col_blocks
    fetches = 8
    batch = slot_count // fetches

    def build():
        def body(rows_hbm, cols_hbm, live_hbm, blocks_hbm, _, out_ref, rows_ref, cols_ref, live_ref,
                 seen_ref, held_ref, acc_ref, small_sem, sem):
            small = [
                pltpu.make_async_copy(rows_hbm, rows_ref, small_sem.at[0]),
                pltpu.make_async_copy(cols_hbm, cols_ref, small_sem.at[1]),
                pltpu.make_async_copy(live_hbm, live_ref, small_sem.at[2]),
            ]
            copies = [
                pltpu.make_async_copy(
                    blocks_hbm.at[pl.ds(f * batch, batch)], held_ref.at[pl.ds(f * batch, batch)], sem.at[f]
                )
                for f in range(fetches)
            ]
            for copy in small + copies:
                copy.start()

            def clear(i, carry):
                for j in range(col_blocks):
                    seen_ref[i * col_blocks + j] = -1
                return carry

            lax.fori_loop(0, row_blocks, clear, 0)
            for copy in small:
                copy.wait()

            def add(k, carry):
                row = rows_ref[0, k]
                col = cols_ref[0, k]
                cell = row * col_blocks + col
                device, inner = split(row, own_blocks)
                at = pl.multiple_of((place(device) * own_blocks + inner) * bs, bs)
                q, b = split(col, share_blocks)
                lane = pl.multiple_of(b * bs, bs)

                @pl.when(live_ref[0, k] == 1)
                def _():
                    seen = seen_ref[cell]

                    @pl.when(seen == -1)
                    def _():
                        seen_ref[cell] = -2
                        out_ref[q, pl.ds(at, bs), pl.ds(lane, bs)] = held_ref[k]

                    @pl.when(seen == -2)
                    def _():
                        seen_ref[cell] = k
                        total = out_ref[q, pl.ds(at, bs), pl.ds(lane, bs)].astype(F32) + held_ref[k].astype(F32)
                        acc_ref[k] = total
                        out_ref[q, pl.ds(at, bs), pl.ds(lane, bs)] = total.astype(BF)

                    @pl.when(seen >= 0)
                    def _():
                        total = acc_ref[seen] + held_ref[k].astype(F32)
                        acc_ref[seen] = total
                        out_ref[q, pl.ds(at, bs), pl.ds(lane, bs)] = total.astype(BF)

                return carry

            for f in range(fetches):
                copies[f].wait()
                lax.fori_loop(f * batch, (f + 1) * batch, add, 0, unroll=4)

        def clear_body(out_ref):
            def clear(i, carry):
                at = pl.multiple_of(i * bs, bs)
                for q in range(windows):
                    out_ref[q, pl.ds(at, bs), :] = jnp.zeros((bs, share), BF)
                return carry

            lax.fori_loop(0, row_blocks, clear, 0)

        empty = kernel(
            clear_body, pltpu.VMEM((windows, wrows, share), BF), 0, in_specs=[],
            cost=cost_of(0, wrows * sources * 2),
        )()
        empty = pltpu.with_memory_space_constraint(empty, pltpu.VMEM)
        built = kernel(
            body, pltpu.VMEM((windows, wrows, share), BF), 5, in_specs=[hbm] * 4 + [vmem], aliases={4: 0},
            scratch=[pltpu.SMEM((1, slot_count), jnp.int32)] * 3 + [
                pltpu.SMEM((cells,), jnp.int32),
                pltpu.VMEM((slot_count, bs, bs), BF),
                pltpu.VMEM((slot_count, bs, bs), F32),
                pltpu.SemaphoreType.DMA((3,)),
                pltpu.SemaphoreType.DMA((fetches,)),
            ],
            cost=cost_of(0, wrows * sources * 6),
        )(
            *[
                pltpu.with_memory_space_constraint(x, pltpu.HBM)
                for x in (block_rows, block_cols, block_live, blocks)
            ],
            empty,
        )
        return pltpu.with_memory_space_constraint(built, pltpu.VMEM)

    def gather(piece, last=None):
        held = {0: piece}
        held[1] = xor_permute(piece, "src", groups, 1)
        for k in range(2, groups, 2):
            held[k] = xor_permute(piece, "src", groups, k)
        for k in range(2, groups, 2):
            held[k + 1] = xor_permute(held[k], "src", groups, 1)
        if last is not None:
            for k in range(3, groups, 2):
                held[k] = after(held[k], last)

        def body(here, *refs):
            for k in range(groups):
                at = pl.multiple_of(place(here[3] ^ k) * own_rows, own_rows)
                refs[-1][:, pl.ds(at, own_rows)] = refs[k][...]

        return kernel(body, sds((ds, wrows), BF), groups, placed=True)(
            *[held[k] for k in range(groups)]
        )

    width = share // PARTS
    chunks = [(i, slice(h * width, (h + 1) * width)) for i in range(pairs) for h in range(PARTS)]
    last = len(chunks) - 1
    quarter = cost_of(2 * ds * wrows * share, wrows * share * 2)

    def adjoint_part(sent, chunk, parity, arrived=None):
        index, lanes = chunk

        def body(here, z_ref, g_ref, *refs):
            product = jnp.dot(
                z_ref[...], g_ref[2 * index + here[parity], :, lanes], preferred_element_type=F32
            )
            if arrived is None:
                refs[0][...] = product.astype(BF)
            else:
                product = product + refs[0][...].astype(F32)
                refs[1][...] = product.astype(BF)
                refs[2][...] = product

        more = () if arrived is None else (arrived,)
        shape = sds((ds, width), BF)
        return kernel(
            body, (shape, sds((ds, width))) if more else shape,
            2 + len(more), placed=True, cost=quarter,
        )(sent, matrix, *more)

    def adjoint(sent):
        away, arrived, mine, theirs = [], [], [], []

        def ahead(j):
            z = sent if j < 2 else after(sent, mine[j - 2])
            away.append(adjoint_part(z, chunks[j], 1))
            arrived.append(xor_permute(away[j], "tm", windows, 1))

        ahead(0)
        for j in range(last + 1):
            if j < last:
                ahead(j + 1)
            total, own = adjoint_part(sent, chunks[j], 0, after(arrived[j], away[-1]))
            bit = 2
            while bit * 2 < windows:
                total, own = add(own, xor_permute(total, "tm", windows, bit))
                bit *= 2
            mine.append(own)
            theirs.append(xor_permute(total, "tm", windows, bit))
        return mine, theirs

    def add(a, b):
        def body(a_ref, b_ref, sent_ref, own_ref):
            total = a_ref[...] + b_ref[...].astype(F32)
            sent_ref[...] = total.astype(BF)
            own_ref[...] = total

        return kernel(body, (sds((ds, width), BF), sds((ds, width))), 2)(a, b)

    def scale(a, b, chunk):
        index, lanes = chunk

        def body(here, a_ref, b_ref, gain_ref, out_ref):
            gain = gain_ref[2 * index + here[0], :, lanes]
            total = a_ref[...] + b_ref[...].astype(F32)
            out_ref[...] = (gain * (gain * total)).astype(BF)

        return kernel(body, sds((ds, width), BF), 3, placed=True)(a, b, gain_rows)

    def own_share(mine, theirs):
        count = len(chunks)

        def body(here, *refs):
            gain_ref, s_ref, gamma_ref = refs[2 * count:]
            for i in range(pairs):

                @pl.when(here[2] == i)
                def _():
                    gamma = jnp.zeros((1, ds), F32)
                    for h in range(PARTS):
                        lanes = slice(h * width, (h + 1) * width)
                        j = i * PARTS + h
                        total = refs[j][...] + refs[count + j][...].astype(F32)
                        steepest = jnp.transpose(gain_ref[2 * i + here[0], :, lanes] * total)
                        s_ref[lanes, :] = steepest
                        gamma = gamma + rows_sum(steepest * steepest)
                    gamma_ref[...] = jnp.broadcast_to(gamma, (8, ds))

        return kernel(body, (sds((share, ds)), sds((8, ds))), 2 * count + 1, placed=True)(*mine, *theirs, gain_rows)

    half_rows = wrows // 2

    def forward_part(scaled, chunk, parities, before=None):
        index, lanes = chunk

        def body(here, g_ref, *refs):
            total = None
            for s_ref, parity in zip(refs, parities):
                product = lax.dot_general(
                    s_ref[...], g_ref[2 * index + here[parity], :, lanes], (((1,), (1,)), ((), ())),
                    preferred_element_type=F32,
                )
                total = product if total is None else total + product
            if before is not None:
                total = total + refs[len(parities)][...]
            refs[-1][...] = total

        more = () if before is None else (before,)
        return kernel(
            body, sds((ds, wrows)), 1 + len(scaled) + len(more), placed=True, cost=quarter
        )(matrix, *scaled, *more)

    steps = groups // 2
    near = steps // 2
    part_rows = half_rows // 2

    def forward_last(scaled, chunk, before, dtype):
        index, lanes = chunk

        def body(here, g_ref, s_ref, before_ref, far_ref, near_ref, keep_ref):
            own = here[3] & 1
            group = (here[3] >> 1) // near if near > 1 else here[3] >> 1
            away = (1 - own) * half_rows
            for at, out_ref in (
                (away + (1 - group) * part_rows, far_ref),
                (away + group * part_rows, near_ref),
                (own * half_rows, keep_ref),
            ):
                rows = pl.ds(pl.multiple_of(at, own_rows), out_ref.shape[1])
                product = lax.dot_general(
                    s_ref[...], g_ref[2 * index + here[1], rows, lanes], (((1,), (1,)), ((), ())),
                    preferred_element_type=F32,
                )
                out_ref[...] = (product + before_ref[:, rows]).astype(out_ref.dtype)

        return kernel(
            body,
            (sds((ds, part_rows), dtype), sds((ds, part_rows), dtype), sds((ds, half_rows))),
            3, placed=True, cost=quarter,
        )(matrix, scaled, before)

    def pair_sums(arrived, keep, dtype, ks):
        def body(here, arrived_ref, keep_ref, *out_refs):
            for k, out_ref in zip(ks, out_refs):
                block = (here[3] >> 1) ^ k
                inner = pl.multiple_of((block & (near - 1)) * own_rows, own_rows)
                at = pl.multiple_of(block * own_rows, own_rows)
                total = keep_ref[:, pl.ds(at, own_rows)] + arrived_ref[:, pl.ds(inner, own_rows)].astype(F32)
                out_ref[...] = total.astype(out_ref.dtype)

        return kernel(body, tuple(sds((ds, own_rows), dtype if k else F32) for k in ks), 2, placed=True)(arrived, keep)

    def scatter(far, close, keep, dtype, beside):
        far = xor_permute(far, "src", groups, 1)
        close = xor_permute(close, "src", groups, 1)
        sums = list(pair_sums(after(far, beside), keep, dtype, range(near, steps)))
        sums = [xor_permute(x, "src", groups, 2 * k) for k, x in zip(range(near, steps), sums)]
        mine = list(pair_sums(close, keep, dtype, range(near)))
        return mine[:1] + [xor_permute(x, "src", groups, 2 * k) for k, x in zip(range(1, near), mine[1:])] + sums

    def forward(mine, theirs, out):
        total = None
        for j in range(last + 1):
            scaled = scale(mine[j], after(theirs[j], mine[-1]), chunks[j])
            other = xor_permute(scaled, "tm", windows, 1)
            if j < last:
                total = forward_part([scaled, other], chunks[j], [0, 1], total)
            else:
                total = forward_part([scaled], chunks[j], [0], total)
                far, close, keep = forward_last(other, chunks[j], total, out)
        steepest, gamma = own_share(mine[:-1] + [after(mine[-1], far)], theirs)
        return steepest, gamma, scatter(far, close, keep, out, gamma)

    def rows_sum(x):
        return jnp.sum(x, axis=0, keepdims=True)

    def sum_blocks(ref, height, count):
        total = ref[0:height, :].astype(F32)
        for b in range(1, count):
            total = total + ref[b * height:(b + 1) * height, :].astype(F32)
        return total

    parts = groups // 2

    def sum_parts(refs):
        total = refs[0][...]
        for ref in refs[1:]:
            total = total + ref[...].astype(F32)
        return total

    def first_norm_body(*refs):
        w_ref, gamma_ref, q_ref, scal_ref = refs[parts:]
        image = jnp.transpose(w_ref[...] * sum_parts(refs[:parts]))
        q_ref[...] = image
        zero = jnp.zeros((6, ds), F32)
        tile = jnp.concatenate([gamma_ref[0:1, :], rows_sum(image * image), zero], axis=0)
        repeat(tile, scal_ref, devices)

    def first_step_body(scal_ref, q_ref, r_ref, w_ref, sent_ref, r_out, keep_ref):
        tile = sum_blocks(scal_ref, 8, devices)
        keep_ref[...] = tile
        step = tile[0:1, :] / (tile[1:2, :] + EPSILON)
        residual = r_ref[...] - step * q_ref[...]
        r_out[...] = residual
        sent_ref[...] = (w_ref[...] * jnp.transpose(residual)).astype(BF)

    def last_norm_body(*refs):
        w_ref, gamma_ref, q_ref, r_ref, a_ref, scal_ref = refs[parts:]
        image = jnp.transpose(w_ref[...] * sum_parts(refs[:parts]))
        a_ref[...] = image
        before, residual = q_ref[...], r_ref[...]
        rows = [
            gamma_ref[0:1, :],
            rows_sum(image * image),
            rows_sum(image * before),
            rows_sum(image * residual),
            rows_sum(before * residual),
            rows_sum(residual * residual),
            jnp.zeros((2, ds), F32),
        ]
        repeat(jnp.concatenate(rows, axis=0), scal_ref, devices)

    def last_step_body(scal_ref, keep_ref, q_ref, a_ref, r_ref, s0_ref, s1_ref, x_ref, r_out, m_ref):
        tile = sum_blocks(scal_ref, 8, devices)
        gamma, norm = keep_ref[0:1, :], keep_ref[1:2, :]
        step = gamma / (norm + EPSILON)
        gamma_next = tile[0:1, :]
        beta = gamma_next / (gamma + EPSILON)
        image_norm = tile[1:2, :] + 2.0 * beta * tile[2:3, :] + beta * beta * norm
        step_next = gamma_next / (image_norm + EPSILON)
        cross = tile[3:4, :] + beta * tile[4:5, :]
        square = tile[5:6, :]
        m_ref[0:1, :] = square / total_rows
        m_ref[1:2, :] = (
            square - 2.0 * step_next * cross + step_next * step_next * image_norm
        ) / total_rows
        r_out[...] = r_ref[...] - step_next * (a_ref[...] + beta * q_ref[...])
        x_ref[...] = (step + step_next * beta) * s0_ref[...] + step_next * s1_ref[...]

    def everywhere(tile):
        return lax.all_to_all(tile, ("src", "tm"), 0, 0, tiled=True)

    square_sds = sds((own_rows, ds))
    scal_sds = sds((devices * 8, ds))
    matrix = build()
    mine, theirs = adjoint(gather(sent, matrix))
    steepest0, gamma0, image = forward(mine, theirs, F32)
    image0, sums = kernel(first_norm_body, (square_sds, scal_sds), parts + 2)(*image, row_weight, gamma0)
    sums = everywhere(sums)
    sent, residual1, kept = kernel(
        first_step_body, (sds((ds, own_rows), BF), square_sds, sds((8, ds))), 4
    )(sums, image0, residual0, row_weight)
    mine, theirs = adjoint(gather(sent))
    steepest1, gamma1, image = forward(mine, theirs, F32)
    image1, sums = kernel(
        last_norm_body, (square_sds, scal_sds), parts + 4
    )(*image, row_weight, gamma1, image0, residual1)
    sums = everywhere(sums)
    solved, residual, misfit = kernel(
        last_step_body, (sds((share, ds)), square_sds, sds((ITERS, ds))), 7
    )(sums, kept, image0, image1, residual1, steepest0, steepest1)
    return solved, residual[None], misfit


def solution(mesh):
    placed = (
        P("tm", "src", None, None),
        P("tm", "src"),
        P("tm", "src"),
        P("tm", "src"),
        P("tm", "src", None),
        P("tm", "src"),
        P("src"),
    )
    return jax.shard_map(
        shards,
        mesh=mesh,
        in_specs=placed,
        out_specs=(P(("src", "tm"), None), P("tm", "src", None), P()),
        check_vma=False,
    )
```

```python
import jax
import jax.numpy as jnp
from jax import lax
from jax.experimental import pallas as pl
from jax.experimental.pallas import tpu as pltpu
from jax.sharding import PartitionSpec as P


ITERS = 2
EPSILON = 1e-06
PARTS = 2
BF = jnp.bfloat16
F32 = jnp.float32


def params(mib):
    return pltpu.CompilerParams(vmem_limit_bytes=mib << 20)


def sds(shape, dtype=F32):
    return jax.ShapeDtypeStruct(shape, dtype)


def xor_permute(array, axis, count, bit):
    return lax.ppermute(array, axis, [(i, i ^ bit) for i in range(count)])


def shards(green, block_rows, block_cols, block_live, data, row_weight, source_gain):
    blocks = green[0]
    slot_count, bs, _ = blocks.shape
    own_rows, ds = data.shape[1], data.shape[2]
    groups = lax.axis_size("src")
    windows = lax.axis_size("tm")
    devices = groups * windows
    sources = source_gain.shape[0]
    wrows = own_rows * groups
    row_blocks = wrows // bs
    col_blocks = sources // bs
    share = sources // windows
    share_blocks = share // bs
    total_rows = wrows * windows
    pairs = windows // 2

    def where():
        tm_index = lax.axis_index("tm")
        return [tm_index & 1, 1 - (tm_index & 1), tm_index >> 1, lax.axis_index("src")]

    gain_rows = source_gain.reshape(windows, 1, share)
    vmem = pl.BlockSpec(memory_space=pltpu.VMEM)
    hbm = pl.BlockSpec(memory_space=pltpu.HBM)

    def kernel(body, out_shape, count, placed=False, in_specs=None, scratch=(), mib=12, cost=None,
               aliases=None):
        def run(*refs):
            body(where(), *refs)

        return pl.pallas_call(
            run if placed else body,
            out_shape=out_shape,
            in_specs=[vmem] * count if in_specs is None else in_specs,
            out_specs=jax.tree.map(lambda _: vmem, out_shape),
            scratch_shapes=scratch,
            input_output_aliases=aliases or {},
            compiler_params=params(mib),
            cost_estimate=cost,
        )

    def after(array, *others):
        return lax.optimization_barrier((array, *others))[0]

    def cost_of(flops, nbytes):
        return pl.CostEstimate(flops=flops, transcendentals=0, bytes_accessed=nbytes)

    def repeat(tile, out_ref, count):
        height = tile.shape[0]
        for b in range(count):
            out_ref[b * height:(b + 1) * height, :] = tile

    def pre_body(data_hbm, w_hbm, sent_ref, r_ref, data_ref, w_ref, sem):
        copies = [
            pltpu.make_async_copy(data_hbm, data_ref, sem.at[0]),
            pltpu.make_async_copy(w_hbm, w_ref, sem.at[1]),
        ]
        for copy in copies:
            copy.start()
        for copy in copies:
            copy.wait()
        residual = w_ref[...] * jnp.transpose(data_ref[...])
        sent_ref[...] = (w_ref[...] * residual).astype(BF)
        r_ref[...] = jnp.transpose(residual)

    sent, residual0 = kernel(
        pre_body, (sds((ds, own_rows), BF), sds((own_rows, ds))), 2, in_specs=[hbm, hbm],
        scratch=[
            pltpu.VMEM((own_rows, ds), F32), pltpu.VMEM((1, own_rows), F32),
            pltpu.SemaphoreType.DMA((2,)),
        ],
    )(*[pltpu.with_memory_space_constraint(x, pltpu.HBM) for x in (data[0], row_weight)])

    own_blocks = own_rows // bs

    def place(device):
        return (device & 1) * (groups // 2) + (device >> 1)

    def split(x, size):
        assert size & (size - 1) == 0
        return x >> (size.bit_length() - 1), x & (size - 1)

    cells = row_blocks * col_blocks
    fetches = 8
    batch = slot_count // fetches

    def build():
        def body(rows_hbm, cols_hbm, live_hbm, blocks_hbm, _, out_ref, rows_ref, cols_ref, live_ref,
                 seen_ref, held_ref, acc_ref, small_sem, sem):
            small = [
                pltpu.make_async_copy(rows_hbm, rows_ref, small_sem.at[0]),
                pltpu.make_async_copy(cols_hbm, cols_ref, small_sem.at[1]),
                pltpu.make_async_copy(live_hbm, live_ref, small_sem.at[2]),
            ]
            copies = [
                pltpu.make_async_copy(
                    blocks_hbm.at[pl.ds(f * batch, batch)], held_ref.at[pl.ds(f * batch, batch)], sem.at[f]
                )
                for f in range(fetches)
            ]
            for copy in small + copies:
                copy.start()

            def clear(i, carry):
                for j in range(col_blocks):
                    seen_ref[i * col_blocks + j] = -1
                return carry

            lax.fori_loop(0, row_blocks, clear, 0)
            for copy in small:
                copy.wait()

            def add(k, carry):
                row = rows_ref[0, k]
                col = cols_ref[0, k]
                cell = row * col_blocks + col
                device, inner = split(row, own_blocks)
                at = pl.multiple_of((place(device) * own_blocks + inner) * bs, bs)
                q, b = split(col, share_blocks)
                lane = pl.multiple_of(b * bs, bs)

                live = live_ref[0, k] == 1
                seen = seen_ref[cell]

                @pl.when(live & (seen == -1))
                def _():
                    seen_ref[cell] = -2
                    out_ref[q, pl.ds(at, bs), pl.ds(lane, bs)] = held_ref[k]

                @pl.when(live & (seen != -1))
                def _():
                    @pl.when(seen == -2)
                    def _():
                        seen_ref[cell] = k
                        total = out_ref[q, pl.ds(at, bs), pl.ds(lane, bs)].astype(F32) + held_ref[k].astype(F32)
                        acc_ref[k] = total
                        out_ref[q, pl.ds(at, bs), pl.ds(lane, bs)] = total.astype(BF)

                    @pl.when(seen >= 0)
                    def _():
                        total = acc_ref[seen] + held_ref[k].astype(F32)
                        acc_ref[seen] = total
                        out_ref[q, pl.ds(at, bs), pl.ds(lane, bs)] = total.astype(BF)

                return carry

            for f in range(fetches):
                copies[f].wait()
                lax.fori_loop(f * batch, (f + 1) * batch, add, 0, unroll=8)

        def clear_body(out_ref):
            def clear(i, carry):
                at = pl.multiple_of(i * bs, bs)
                for q in range(windows):
                    out_ref[q, pl.ds(at, bs), :] = jnp.zeros((bs, share), BF)
                return carry

            lax.fori_loop(0, row_blocks, clear, 0)

        empty = kernel(
            clear_body, pltpu.VMEM((windows, wrows, share), BF), 0, in_specs=[],
            cost=cost_of(0, wrows * sources * 2),
        )()
        empty = pltpu.with_memory_space_constraint(empty, pltpu.VMEM)
        built = kernel(
            body, pltpu.VMEM((windows, wrows, share), BF), 5, in_specs=[hbm] * 4 + [vmem], aliases={4: 0},
            scratch=[pltpu.SMEM((1, slot_count), jnp.int32)] * 3 + [
                pltpu.SMEM((cells,), jnp.int32),
                pltpu.VMEM((slot_count, bs, bs), BF),
                pltpu.VMEM((slot_count, bs, bs), F32),
                pltpu.SemaphoreType.DMA((3,)),
                pltpu.SemaphoreType.DMA((fetches,)),
            ],
            cost=cost_of(0, wrows * sources * 6),
        )(
            *[
                pltpu.with_memory_space_constraint(x, pltpu.HBM)
                for x in (block_rows, block_cols, block_live, blocks)
            ],
            empty,
        )
        return pltpu.with_memory_space_constraint(built, pltpu.VMEM)

    def gather(piece, last=None):
        held = {0: piece}
        held[1] = xor_permute(piece, "src", groups, 1)
        for k in range(2, groups, 2):
            held[k] = xor_permute(piece, "src", groups, k)
        for k in range(2, groups, 2):
            held[k + 1] = xor_permute(held[k], "src", groups, 1)
        if last is not None:
            for k in range(3, groups, 2):
                held[k] = after(held[k], last)

        def body(here, *refs):
            for k in range(groups):
                at = pl.multiple_of(place(here[3] ^ k) * own_rows, own_rows)
                refs[-1][:, pl.ds(at, own_rows)] = refs[k][...]

        return kernel(body, sds((ds, wrows), BF), groups, placed=True)(
            *[held[k] for k in range(groups)]
        )

    width = share // PARTS
    chunks = [(i, slice(h * width, (h + 1) * width)) for i in range(pairs) for h in range(PARTS)]
    last = len(chunks) - 1
    quarter = cost_of(2 * ds * wrows * share, wrows * share * 2)

    def adjoint_part(sent, chunk, parity, arrived=None):
        index, lanes = chunk

        def body(here, z_ref, g_ref, *refs):
            product = jnp.dot(
                z_ref[...], g_ref[2 * index + here[parity], :, lanes], preferred_element_type=F32
            )
            if arrived is None:
                refs[0][...] = product.astype(BF)
            else:
                product = product + refs[0][...].astype(F32)
                refs[1][...] = product.astype(BF)
                refs[2][...] = product

        more = () if arrived is None else (arrived,)
        shape = sds((ds, width), BF)
        return kernel(
            body, (shape, sds((ds, width))) if more else shape,
            2 + len(more), placed=True, cost=quarter,
        )(sent, matrix, *more)

    def adjoint(sent):
        away, arrived, mine, theirs = [], [], [], []

        def ahead(j):
            z = sent if j < 2 else after(sent, mine[j - 2])
            away.append(adjoint_part(z, chunks[j], 1))
            arrived.append(xor_permute(away[j], "tm", windows, 1))

        ahead(0)
        for j in range(last + 1):
            if j < last:
                ahead(j + 1)
            total, own = adjoint_part(sent, chunks[j], 0, after(arrived[j], away[-1]))
            bit = 2
            while bit * 2 < windows:
                total, own = add(own, xor_permute(total, "tm", windows, bit))
                bit *= 2
            mine.append(own)
            theirs.append(xor_permute(total, "tm", windows, bit))
        return mine, theirs

    def add(a, b):
        def body(a_ref, b_ref, sent_ref, own_ref):
            total = a_ref[...] + b_ref[...].astype(F32)
            sent_ref[...] = total.astype(BF)
            own_ref[...] = total

        return kernel(body, (sds((ds, width), BF), sds((ds, width))), 2)(a, b)

    def scale(a, b, chunk):
        index, lanes = chunk

        def body(here, a_ref, b_ref, gain_ref, out_ref):
            gain = gain_ref[2 * index + here[0], :, lanes]
            total = a_ref[...] + b_ref[...].astype(F32)
            out_ref[...] = (gain * (gain * total)).astype(BF)

        return kernel(body, sds((ds, width), BF), 3, placed=True)(a, b, gain_rows)

    def own_share(mine, theirs):
        count = len(chunks)

        def body(here, *refs):
            gain_ref, s_ref, gamma_ref = refs[2 * count:]
            for i in range(pairs):

                @pl.when(here[2] == i)
                def _():
                    gamma = jnp.zeros((1, ds), F32)
                    for h in range(PARTS):
                        lanes = slice(h * width, (h + 1) * width)
                        j = i * PARTS + h
                        total = refs[j][...] + refs[count + j][...].astype(F32)
                        steepest = jnp.transpose(gain_ref[2 * i + here[0], :, lanes] * total)
                        s_ref[lanes, :] = steepest
                        gamma = gamma + rows_sum(steepest * steepest)
                    gamma_ref[...] = jnp.broadcast_to(gamma, (8, ds))

        return kernel(body, (sds((share, ds)), sds((8, ds))), 2 * count + 1, placed=True)(*mine, *theirs, gain_rows)

    half_rows = wrows // 2

    def forward_part(scaled, chunk, parities, before=None):
        index, lanes = chunk

        def body(here, g_ref, *refs):
            total = None
            for s_ref, parity in zip(refs, parities):
                product = lax.dot_general(
                    s_ref[...], g_ref[2 * index + here[parity], :, lanes], (((1,), (1,)), ((), ())),
                    preferred_element_type=F32,
                )
                total = product if total is None else total + product
            if before is not None:
                total = total + refs[len(parities)][...]
            refs[-1][...] = total

        more = () if before is None else (before,)
        return kernel(
            body, sds((ds, wrows)), 1 + len(scaled) + len(more), placed=True, cost=quarter
        )(matrix, *scaled, *more)

    steps = groups // 2
    near = steps // 2
    part_rows = half_rows // 2

    def forward_last(scaled, chunk, before, dtype):
        index, lanes = chunk

        def body(here, g_ref, s_ref, before_ref, far_ref, near_ref, keep_ref):
            own = here[3] & 1
            group = (here[3] >> 1) // near if near > 1 else here[3] >> 1
            away = (1 - own) * half_rows
            for at, out_ref in (
                (away + (1 - group) * part_rows, far_ref),
                (away + group * part_rows, near_ref),
                (own * half_rows, keep_ref),
            ):
                rows = pl.ds(pl.multiple_of(at, own_rows), out_ref.shape[1])
                product = lax.dot_general(
                    s_ref[...], g_ref[2 * index + here[1], rows, lanes], (((1,), (1,)), ((), ())),
                    preferred_element_type=F32,
                )
                out_ref[...] = (product + before_ref[:, rows]).astype(out_ref.dtype)

        return kernel(
            body,
            (sds((ds, part_rows), dtype), sds((ds, part_rows), dtype), sds((ds, half_rows))),
            3, placed=True, cost=quarter,
        )(matrix, scaled, before)

    def pair_sums(arrived, keep, dtype, ks):
        def body(here, arrived_ref, keep_ref, *out_refs):
            for k, out_ref in zip(ks, out_refs):
                block = (here[3] >> 1) ^ k
                inner = pl.multiple_of((block & (near - 1)) * own_rows, own_rows)
                at = pl.multiple_of(block * own_rows, own_rows)
                total = keep_ref[:, pl.ds(at, own_rows)] + arrived_ref[:, pl.ds(inner, own_rows)].astype(F32)
                out_ref[...] = total.astype(out_ref.dtype)

        return kernel(body, tuple(sds((ds, own_rows), dtype if k else F32) for k in ks), 2, placed=True)(arrived, keep)

    def scatter(far, close, keep, dtype, beside):
        far = xor_permute(far, "src", groups, 1)
        close = xor_permute(close, "src", groups, 1)
        sums = list(pair_sums(after(far, beside), keep, dtype, range(near, steps)))
        sums = [xor_permute(x, "src", groups, 2 * k) for k, x in zip(range(near, steps), sums)]
        mine = list(pair_sums(close, keep, dtype, range(near)))
        return mine[:1] + [xor_permute(x, "src", groups, 2 * k) for k, x in zip(range(1, near), mine[1:])] + sums

    def forward(mine, theirs, out):
        total = None
        for j in range(last + 1):
            scaled = scale(mine[j], after(theirs[j], mine[-1]), chunks[j])
            other = xor_permute(scaled, "tm", windows, 1)
            if j < last:
                total = forward_part([scaled, other], chunks[j], [0, 1], total)
            else:
                total = forward_part([scaled], chunks[j], [0], total)
                far, close, keep = forward_last(other, chunks[j], total, out)
        steepest, gamma = own_share(mine[:-1] + [after(mine[-1], far)], theirs)
        return steepest, gamma, scatter(far, close, keep, out, gamma)

    def rows_sum(x):
        return jnp.sum(x, axis=0, keepdims=True)

    def sum_blocks(ref, height, count):
        total = ref[0:height, :].astype(F32)
        for b in range(1, count):
            total = total + ref[b * height:(b + 1) * height, :].astype(F32)
        return total

    parts = groups // 2

    def sum_parts(refs):
        total = refs[0][...]
        for ref in refs[1:]:
            total = total + ref[...].astype(F32)
        return total

    def first_norm_body(*refs):
        w_ref, gamma_ref, q_ref, scal_ref = refs[parts:]
        image = jnp.transpose(w_ref[...] * sum_parts(refs[:parts]))
        q_ref[...] = image
        zero = jnp.zeros((6, ds), F32)
        tile = jnp.concatenate([gamma_ref[0:1, :], rows_sum(image * image), zero], axis=0)
        repeat(tile, scal_ref, devices)

    def first_step_body(scal_ref, q_ref, r_ref, w_ref, sent_ref, r_out, keep_ref):
        tile = sum_blocks(scal_ref, 8, devices)
        keep_ref[...] = tile
        step = tile[0:1, :] / (tile[1:2, :] + EPSILON)
        residual = r_ref[...] - step * q_ref[...]
        r_out[...] = residual
        sent_ref[...] = (w_ref[...] * jnp.transpose(residual)).astype(BF)

    def last_norm_body(*refs):
        w_ref, gamma_ref, q_ref, r_ref, a_ref, scal_ref = refs[parts:]
        image = jnp.transpose(w_ref[...] * sum_parts(refs[:parts]))
        a_ref[...] = image
        before, residual = q_ref[...], r_ref[...]
        rows = [
            gamma_ref[0:1, :],
            rows_sum(image * image),
            rows_sum(image * before),
            rows_sum(image * residual),
            rows_sum(before * residual),
            rows_sum(residual * residual),
            jnp.zeros((2, ds), F32),
        ]
        repeat(jnp.concatenate(rows, axis=0), scal_ref, devices)

    def last_step_body(scal_ref, keep_ref, q_ref, a_ref, r_ref, s0_ref, s1_ref, x_ref, r_out, m_ref):
        tile = sum_blocks(scal_ref, 8, devices)
        gamma, norm = keep_ref[0:1, :], keep_ref[1:2, :]
        step = gamma / (norm + EPSILON)
        gamma_next = tile[0:1, :]
        beta = gamma_next / (gamma + EPSILON)
        image_norm = tile[1:2, :] + 2.0 * beta * tile[2:3, :] + beta * beta * norm
        step_next = gamma_next / (image_norm + EPSILON)
        cross = tile[3:4, :] + beta * tile[4:5, :]
        square = tile[5:6, :]
        m_ref[0:1, :] = square / total_rows
        m_ref[1:2, :] = (
            square - 2.0 * step_next * cross + step_next * step_next * image_norm
        ) / total_rows
        r_out[...] = r_ref[...] - step_next * (a_ref[...] + beta * q_ref[...])
        x_ref[...] = (step + step_next * beta) * s0_ref[...] + step_next * s1_ref[...]

    def everywhere(tile):
        return lax.all_to_all(tile, ("src", "tm"), 0, 0, tiled=True)

    square_sds = sds((own_rows, ds))
    scal_sds = sds((devices * 8, ds))
    matrix = build()
    mine, theirs = adjoint(gather(sent, matrix))
    steepest0, gamma0, image = forward(mine, theirs, F32)
    image0, sums = kernel(first_norm_body, (square_sds, scal_sds), parts + 2)(*image, row_weight, gamma0)
    sums = everywhere(sums)
    sent, residual1, kept = kernel(
        first_step_body, (sds((ds, own_rows), BF), square_sds, sds((8, ds))), 4
    )(sums, image0, residual0, row_weight)
    mine, theirs = adjoint(gather(sent))
    steepest1, gamma1, image = forward(mine, theirs, F32)
    image1, sums = kernel(
        last_norm_body, (square_sds, scal_sds), parts + 4
    )(*image, row_weight, gamma1, image0, residual1)
    sums = everywhere(sums)
    solved, residual, misfit = kernel(
        last_step_body, (sds((share, ds)), square_sds, sds((ITERS, ds))), 7
    )(sums, kept, image0, image1, residual1, steepest0, steepest1)
    return solved, residual[None], misfit


def solution(mesh):
    placed = (
        P("tm", "src", None, None),
        P("tm", "src"),
        P("tm", "src"),
        P("tm", "src"),
        P("tm", "src", None),
        P("tm", "src"),
        P("src"),
    )
    return jax.shard_map(
        shards,
        mesh=mesh,
        in_specs=placed,
        out_specs=(P(("src", "tm"), None), P("tm", "src", None), P()),
        check_vma=False,
    )
```
